32 devices in a mesh: rep: 2 (over x), node: 2 (over core), local: 8 (over z, y).
Axes of the slice: x: 2, y: 2, z: 4, core: 2. Of those that a mesh axis runs over, the one named last changes fastest.
Arguments:
- tokens: bfloat16 [1024, 3584], P(('rep', 'node', 'local')), parts along dimension 0, may hold values from -6 to 6
- expert_ids: int32 [1024, 8], P(('rep', 'node', 'local')), parts along dimension 0, may hold values from 0 to 15, all different within a row; in each aligned block of 32 rows (0 to 31, 32 to 63, ...) at most 32 rows name the same one
- route_weights: bfloat16 [1024, 8], P(('rep', 'node', 'local')), parts along dimension 0, may hold values from 0.099609375 to 1
- w_up: bfloat16 [16, 3584, 1024], P(('node', 'local')), may hold values from -0.09375 to 0.09375
- w_down: bfloat16 [16, 1024, 3584], P(('node', 'local')), may hold values from -0.1875 to 0.1875
Outputs:
- mixed: bfloat16 [1024, 3584], P(('rep', 'node', 'local')), parts along dimension 0
The draws below stay inside these ranges and needn't reach their ends.
There are 2 independent parts, one for each index of `rep`. The reference program is written for one: setup_inputs(seed, part) draws one part's arguments, and reference() takes and returns one part's arrays. A program takes and returns all parts, laid end to end along the dimension named above; an argument that names none is the same for every part. Nothing has to cross between parts.
Inputs may be any that keep to these rules, and one draw needn't show every extreme that they name: `expert_ids`: the 8 experts of a token differ; in each aligned block of 32 rows (the rows of one device) no expert is named by more than 32 rows.
All inputs are finite; a program needn't handle non-finite values.
Results may differ from the reference program's by a relative error of at most 0.0058.
Values may be sent and summed in bfloat16 or wider, within the bound.
A program may use at most 64 MiB of HBM per device.

```python
import math
import jax
import jax.numpy as jnp
import numpy as np
from jax import lax

D = 3584
FF = 1024
TOP = 8
TOK_DEV = 32
EXPERTS = 16
MOST = 32
TOKENS = 512


def block_levels(key, shape, cuts, least, largest):
    loudness = 1.0
    for position, parts in cuts:
        steps = jax.random.uniform(jax.random.fold_in(jax.random.fold_in(key, 6), position), (parts,), jnp.float32, least / len(cuts), largest / len(cuts))
        loudness = loudness * jnp.repeat(jnp.exp(steps), shape[position] // parts).reshape((-1,) + (1,) * (len(shape) - 1 - position))
    return loudness


def shared_out(own_key, own, number, rows, amount, top, most, slope):
    order = jax.random.permutation(own_key, amount)
    packed, common = portions_of(amount, rows * top, most, slope, True), portions_of(amount, rows * top, most, slope, False)
    places = jnp.arange(amount)

    def named(tallies, rotation):
        used = int((tallies > 0).sum())
        fixed = max(1, used // 4)
        passed = fixed + (places - fixed + rotation * (used - fixed)) % max(1, amount - fixed)
        return jnp.zeros((amount,), jnp.int32).at[order[jnp.where(places < fixed, places, passed)]].set(jnp.asarray(tallies, jnp.int32))

    tallies = jnp.where(number % 4 == 0, named(packed, number // 4), named(common, number - number // 4 - 1))
    mixed = jax.random.permutation(jax.random.fold_in(own, 3), amount)
    donor, sink = mixed[0:amount // 2 * 2:2], mixed[1:amount // 2 * 2:2]
    slack = jnp.minimum(tallies[donor] - 1, most - tallies[sink]) // 2
    slack = jnp.where((donor == order[0]) | (sink == order[0]) | (tallies[sink] == 0), 0, jnp.maximum(slack, 0))
    passed = jax.random.randint(jax.random.fold_in(own, 4), (amount // 2,), 0, 1 << 20) % (slack + 1)
    tallies = tallies.at[donor].add(-passed).at[sink].add(passed)
    labels = jnp.searchsorted(jnp.cumsum(tallies), jnp.arange(rows * top), side="right").astype(jnp.int32)
    grid = labels.reshape(top, rows).T
    grid = grid[jax.random.permutation(jax.random.fold_in(own, 1), rows)]
    rotation = jax.random.randint(jax.random.fold_in(own, 2), (rows, 1), 0, top)
    return jnp.take_along_axis(grid, (jnp.arange(top)[None, :] + rotation) % top, axis=1)


def portions_of(number_of, total, reach, skew, full):
    portions = [(1 << 20) // math.isqrt(grade ** skew) + 1 for grade in range(1, number_of + 1)]
    largest = reach if full else min(reach, max(-(-total // number_of), total * portions[0] // sum(portions)))
    least = 1 if total - largest >= number_of - 1 else 0
    holding, rest = [largest] + [least] * (number_of - 1), total - largest - least * (number_of - 1)
    while rest > 0:
        candidates = [i for i in range(1, number_of) if holding[i] < largest] or [i for i in range(1, number_of) if holding[i] < reach]
        pool, remaining = sum([portions[i] for i in candidates]), rest
        for i in candidates:
            extra = min(reach - holding[i], max(1, remaining * portions[i] // pool), rest)
            holding[i] = holding[i] + extra
            rest = rest - extra
    return np.array(holding)


def bell_draw(own_key, shape, scale, most, split=(), kind=jnp.bfloat16):
    values = scale * jax.random.normal(own_key, shape, jnp.float32)
    if split:
        values = values * block_levels(own_key, shape, split, -0.22, 0.18)
    return jnp.clip(values, -most, most).astype(kind)


def setup_inputs(seed: int = 0, part: int = 0) -> dict:
    keys = jax.random.split(jax.random.key(seed), 6)
    own_keys = jax.random.split(jax.random.fold_in(keys[5], part), 6)
    tokens = bell_draw(own_keys[0], (TOKENS, D), 1.0, 6.0, ((0, 16),))
    expert_ids_keys = jax.random.split(jax.random.fold_in(own_keys[1], 1), TOKENS // TOK_DEV)
    expert_ids_turns = jax.random.permutation(jax.random.fold_in(own_keys[1], 3), TOKENS // TOK_DEV)
    expert_ids = jax.vmap(lambda own, number: shared_out(jax.random.fold_in(own_keys[1], 2), own, number, TOK_DEV, EXPERTS, TOP, MOST, 2))(expert_ids_keys, expert_ids_turns).reshape((TOKENS, TOP))
    route_weights = jnp.clip(0.099609375 + 0.9003906 * jax.random.uniform(own_keys[2], (TOKENS, TOP), jnp.float32) ** block_levels(own_keys[2], (TOKENS, TOP), ((0, 16),), -0.2, 0.2), 0.099609375, 1.0).astype(jnp.bfloat16)
    w_up = bell_draw(keys[3], (EXPERTS, D, FF), D ** -0.5, 0.09375, ((0, 16),))
    w_down = bell_draw(keys[4], (EXPERTS, FF, D), FF ** -0.5, 0.1875, ((0, 16),))
    return dict(tokens=tokens, expert_ids=expert_ids, route_weights=route_weights, w_up=w_up, w_down=w_down)


def reference(tokens, expert_ids, route_weights, w_up, w_down):
    total = tokens.shape[0]
    top = expert_ids.shape[1]
    flat_ids = expert_ids.reshape(-1)
    flat_weights = route_weights.reshape(-1).astype(jnp.float32)
    bound = EXPERTS * MOST
    filler = total * top

    def one_expert(carry, inputs):
        index, up, down = inputs
        picks = jnp.nonzero(flat_ids == index, size=bound, fill_value=filler)[0].astype(jnp.int32)
        valid = picks < filler
        token_rows = jnp.where(valid, picks // top, 0).astype(jnp.int32)
        rows = tokens[token_rows]
        hidden = jax.nn.silu(jnp.dot(rows, up, preferred_element_type=jnp.float32)).astype(jnp.bfloat16)
        answer = jnp.dot(hidden, down, preferred_element_type=jnp.float32).astype(jnp.bfloat16)
        scale = jnp.where(valid, flat_weights[jnp.minimum(picks, filler - 1)], 0.0)
        return carry.at[token_rows].add(scale[:, None] * answer.astype(jnp.float32)), None

    start = jnp.zeros((total, tokens.shape[1]), jnp.float32)
    result, _ = lax.scan(one_expert, start, (jnp.arange(EXPERTS, dtype=jnp.int32), w_up, w_down))
    return result.astype(jnp.bfloat16)
```

```python
import functools
import jax
import jax.numpy as jnp
from jax import lax
from jax.experimental import pallas as pl
from jax.experimental.pallas import tpu as pltpu
from jax.sharding import PartitionSpec as P

MESH = pl.DeviceIdType.MESH
LANES = 128


def moe_kernel(sizes, x_hbm, dense_hbm, up_hbm, down_hbm, out_ref,
               xg, wg, up, down, acc, hid, wcol,
               psend, pown, precv, ysend, yown, yrecv, zsend, zown, zrecv,
               own_sem, up_sem, down_sem,
               gz_s, gz_r, gy_s, gy_r, gp_s, gp_r,
               rp_s, rp_r, ry_s, ry_r, rz_s, rz_r):
    rows, major, chunks, width = sizes
    core = lax.axis_index("node")
    local = lax.axis_index("local")
    z, y = local // 2, lax.rem(local, 2)
    col_rows = major * rows
    half = 2 * col_rows

    def at_z(d):
        return {"local": lax.rem(z + d, major) * 2 + y}

    at_y = {"local": z * 2 + (1 - y)}
    at_p = {"node": 1 - core}

    barrier = pltpu.get_barrier_semaphore()
    peers = [at_z(d) for d in range(1, major)] + [at_y, at_p]
    for peer in peers:
        pl.semaphore_signal(barrier, inc=1, device_id=peer, device_id_type=MESH)

    def rows_of(c, yy, zz):
        return pl.multiple_of(c * half + yy * col_rows + zz * rows, rows)

    mine = rows_of(core, y, z)
    own_x = pltpu.make_async_copy(x_hbm, xg.at[pl.ds(mine, rows), :], own_sem.at[0])
    own_w = pltpu.make_async_copy(dense_hbm, wg.at[pl.ds(mine, rows), :], own_sem.at[1])
    own_x.start()
    own_w.start()

    def cols(j):
        return pl.ds(pl.multiple_of(j * width, width), width)

    def up_copy(j):
        return pltpu.make_async_copy(up_hbm.at[0, cols(j), :], up.at[cols(j), :], up_sem.at[j])

    def down_copy(j):
        return pltpu.make_async_copy(down_hbm.at[0, :, cols(j)], down.at[:, cols(j)], down_sem.at[j])

    lax.fori_loop(0, chunks, lambda j, _: (up_copy(j).start(), 0)[1], 0)
    lax.fori_loop(0, chunks, lambda j, _: (down_copy(j).start(), 0)[1], 0)

    own_x.wait()
    own_w.wait()
    pl.semaphore_wait(barrier, len(peers))

    def view(start, size, j):
        if j is None:
            return wg.at[pl.ds(start, size), :]
        return xg.at[pl.ds(start, size), cols(j)]

    def idx(j):
        return chunks if j is None else j

    def remote(src, dst, s, r, device):
        return pltpu.make_async_remote_copy(
            src_ref=src, dst_ref=dst, send_sem=s, recv_sem=r, device_id=device, device_id_type=MESH)

    def gz_send(d, j):
        v = view(mine, rows, j)
        return remote(v, v, gz_s.at[d - 1, idx(j)], gz_r.at[d - 1, idx(j)], at_z(d))

    def gz_recv(d, j):
        v = view(rows_of(core, y, lax.rem(z + major - d, major)), rows, j)
        return remote(v, v, gz_s.at[d - 1, idx(j)], gz_r.at[d - 1, idx(j)], at_z(d))

    def gy(which, j):
        v = view(rows_of(core, which, 0), col_rows, j)
        return remote(v, v, gy_s.at[idx(j)], gy_r.at[idx(j)], at_y)

    def gp(k, c, which, j):
        v = view(rows_of(c, which, 0), col_rows, j)
        return remote(v, v, gp_s.at[k, idx(j)], gp_r.at[k, idx(j)], at_p)

    def stage0(j):
        for d in range(1, major):
            gz_send(d, j).start()

    def stage1(j):
        for d in range(1, major):
            gz_recv(d, j).wait_recv()
        gy(y, j).start()
        gp(0, core, y, j).start()

    def stage2(j):
        gy(1 - y, j).wait_recv()
        gp(1, core, 1 - y, j).start()

    def stage3(j):
        gp(0, 1 - core, y, j).wait_recv()
        gp(1, 1 - core, 1 - y, j).wait_recv()

    lax.fori_loop(0, chunks, lambda j, _: (stage0(j), 0)[1], 0)
    stage0(None)

    def gather_step(t, _):
        @pl.when(t < chunks)
        def _():
            stage1(t)

        @pl.when((t >= 1) & (t <= chunks))
        def _():
            stage2(t - 1)

        @pl.when(t >= 2)
        def _():
            j = t - 2
            stage3(j)
            up_copy(j).wait()
            for k in range(2):
                r = pl.ds(k * half, half)
                part = jnp.dot(xg[r, cols(j)], up[cols(j), :], preferred_element_type=jnp.float32)

                @pl.when(j == 0)
                def _():
                    acc[r, :] = part

                @pl.when(j > 0)
                def _():
                    acc[r, :] += part
        return 0

    lax.fori_loop(0, chunks, gather_step, 0)
    stage1(None)
    lax.fori_loop(chunks, chunks + 1, gather_step, 0)
    stage2(None)
    lax.fori_loop(chunks + 1, chunks + 2, gather_step, 0)
    stage3(None)

    for k in range(2):
        r = pl.ds(k * half, half)
        v = acc[r, :]
        hid[r, :] = (v / (1.0 + jnp.exp(-v))).astype(hid.dtype)
    expert = core * (2 * major) + local
    lane = lax.broadcasted_iota(jnp.int32, wg.shape, 1)
    wcol[...] = jnp.sum(jnp.where(lane == expert, wg[...].astype(jnp.float32), 0.0), axis=1, keepdims=True)

    def rp(j):
        return remote(psend.at[:, cols(j)], precv.at[:, cols(j)], rp_s.at[j], rp_r.at[j], at_p)

    def ry(j):
        return remote(ysend.at[:, cols(j)], yrecv.at[:, cols(j)], ry_s.at[j], ry_r.at[j], at_y)

    def rz(d, j):
        src = zsend.at[pl.ds(pl.multiple_of(lax.rem(z + d, major) * rows, rows), rows), cols(j)]
        return remote(src, zrecv.at[d - 1, :, cols(j)], rz_s.at[d - 1, j], rz_r.at[d - 1, j], at_z(d))

    theirs = pl.ds(pl.multiple_of((1 - core) * half, half), half)
    ours = pl.ds(pl.multiple_of(core * half, half), half)
    y_theirs = pl.ds(pl.multiple_of((1 - y) * col_rows, col_rows), col_rows)
    y_ours = pl.ds(pl.multiple_of(y * col_rows, col_rows), col_rows)
    z_ours = pl.ds(pl.multiple_of(z * rows, rows), rows)

    def scatter_step(t, _):
        @pl.when(t < chunks)
        def _():
            j = t
            down_copy(j).wait()
            part = jnp.dot(hid[theirs, :], down[:, cols(j)], preferred_element_type=jnp.float32)
            psend[:, cols(j)] = (part * wcol[theirs, :]).astype(psend.dtype)
            rp(j).start()
            part = jnp.dot(hid[ours, :], down[:, cols(j)], preferred_element_type=jnp.float32)
            pown[:, cols(j)] = part * wcol[ours, :]

        @pl.when((t >= 1) & (t <= chunks))
        def _():
            j = t - 1
            rp(j).wait_recv()
            ysend[:, cols(j)] = (pown[y_theirs, cols(j)] + precv[y_theirs, cols(j)].astype(jnp.float32)).astype(ysend.dtype)
            ry(j).start()
            yown[:, cols(j)] = pown[y_ours, cols(j)] + precv[y_ours, cols(j)].astype(jnp.float32)

        @pl.when((t >= 2) & (t <= chunks + 1))
        def _():
            j = t - 2
            ry(j).wait_recv()
            zsend[:, cols(j)] = (yown[:, cols(j)] + yrecv[:, cols(j)].astype(jnp.float32)).astype(zsend.dtype)
            for d in range(1, major):
                rz(d, j).start()
            zown[:, cols(j)] = yown[z_ours, cols(j)] + yrecv[z_ours, cols(j)].astype(jnp.float32)

        @pl.when(t >= 3)
        def _():
            j = t - 3
            total = zown[:, cols(j)]
            for d in range(1, major):
                rz(d, j).wait_recv()
                total = total + zrecv[d - 1, :, cols(j)].astype(jnp.float32)
            out_ref[:, cols(j)] = total.astype(out_ref.dtype)
        return 0

    lax.fori_loop(0, chunks + 3, scatter_step, 0)

    def drain_gather(j):
        for d in range(1, major):
            gz_send(d, j).wait_send()
        gy(y, j).wait_send()
        gp(0, core, y, j).wait_send()
        gp(1, core, 1 - y, j).wait_send()

    def drain(j, _):
        drain_gather(j)
        rp(j).wait_send()
        ry(j).wait_send()
        for d in range(1, major):
            rz(d, j).wait_send()
        return 0

    drain_gather(None)
    lax.fori_loop(0, chunks, drain, 0)


def fused(tokens, expert_ids, route_weights, w_up, w_down, width=512):
    rows, depth = tokens.shape
    ff = w_up.shape[2]
    experts = lax.axis_size(("node", "local"))
    major = lax.axis_size("local") // 2
    chunks = depth // width
    lanes = -(-experts // LANES) * LANES
    hit = expert_ids[:, :, None] == jnp.arange(lanes, dtype=jnp.int32)
    dense = jnp.sum(jnp.where(hit, route_weights[:, :, None].astype(jnp.float32), 0.0), axis=1).astype(jnp.bfloat16)
    total, col = experts * rows, major * rows
    half = 2 * col
    bf, f32 = jnp.bfloat16, jnp.float32
    dma = pltpu.SemaphoreType.DMA
    return pl.pallas_call(
        functools.partial(moe_kernel, (rows, major, chunks, width)),
        out_shape=jax.ShapeDtypeStruct((rows, depth), bf),
        in_specs=[pl.BlockSpec(memory_space=pl.ANY)] * 4,
        out_specs=pl.BlockSpec(memory_space=pltpu.VMEM),
        scratch_shapes=[
            pltpu.VMEM((total, depth), bf),
            pltpu.VMEM((total, lanes), bf),
            pltpu.VMEM((depth, ff), bf),
            pltpu.VMEM((ff, depth), bf),
            pltpu.VMEM((total, ff), f32),
            pltpu.VMEM((total, ff), bf),
            pltpu.VMEM((total, 1), f32),
            pltpu.VMEM((half, depth), bf),
            pltpu.VMEM((half, depth), f32),
            pltpu.VMEM((half, depth), bf),
            pltpu.VMEM((col, depth), bf),
            pltpu.VMEM((col, depth), f32),
            pltpu.VMEM((col, depth), bf),
            pltpu.VMEM((col, depth), bf),
            pltpu.VMEM((rows, depth), f32),
            pltpu.VMEM((major - 1, rows, depth), bf),
            dma((2,)), dma((chunks,)), dma((chunks,)),
            dma((major - 1, chunks + 1)), dma((major - 1, chunks + 1)),
            dma((chunks + 1,)), dma((chunks + 1,)),
            dma((2, chunks + 1)), dma((2, chunks + 1)),
            dma((chunks,)), dma((chunks,)),
            dma((chunks,)), dma((chunks,)),
            dma((major - 1, chunks)), dma((major - 1, chunks)),
        ],
        compiler_params=pltpu.CompilerParams(
            collective_id=0, has_side_effects=True, vmem_limit_bytes=60 * 1024 * 1024),
    )(tokens, dense, w_up, w_down)


def place_rows(targets, groups, width):
    onehot = (targets[:, None] == jnp.arange(groups, dtype=jnp.int32)[None, :]).astype(jnp.int32)
    before = jnp.cumsum(onehot, axis=0) - onehot
    rank = jnp.sum(before * onehot, axis=1)
    return jnp.where(targets >= 0, targets * width + rank, groups * width)


def per_device(tokens, expert_ids, route_weights, w_up, w_down):
    up_matrix = w_up[0]
    down_matrix = w_down[0]
    rows = tokens.shape[0]
    top = expert_ids.shape[1]
    width_d = tokens.shape[1]
    experts = lax.axis_size(("node", "local"))
    most = max(4, 2 * rows * top // experts)
    slot = place_rows(expert_ids.reshape(-1), experts, most)
    source = tokens[jnp.arange(rows * top, dtype=jnp.int32) // top]
    buffer = jnp.zeros((experts * most, width_d), jnp.bfloat16).at[slot].set(source, mode="drop")
    buffer = buffer.reshape(experts, most, width_d)
    received = lax.all_to_all(buffer, ("node", "local"), split_axis=0, concat_axis=0, tiled=True)
    shape = received.shape
    flat = received.reshape(-1, shape[-1])
    hidden = jax.nn.silu(jnp.dot(flat, up_matrix, preferred_element_type=jnp.float32)).astype(
        jnp.bfloat16
    )
    answer = jnp.dot(hidden, down_matrix, preferred_element_type=jnp.float32).astype(jnp.bfloat16)
    done = answer.reshape(shape)
    returned = lax.all_to_all(
        done, ("node", "local"), split_axis=0, concat_axis=0, tiled=True
    ).reshape(experts * most, width_d)
    picked = returned[jnp.minimum(slot, experts * most - 1)].reshape(rows, top, width_d)
    mixed = jnp.einsum("tk,tkd->td", route_weights, picked, preferred_element_type=jnp.float32)
    return mixed.astype(jnp.bfloat16)


def solution(mesh):
    placed = (
        P(("rep", "node", "local"), None),
        P(("rep", "node", "local"), None),
        P(("rep", "node", "local"), None),
        P(("node", "local"), None, None),
        P(("node", "local"), None, None),
    )

    def body(tokens, expert_ids, route_weights, w_up, w_down):
        experts = mesh.shape["node"] * mesh.shape["local"]
        near_dense = experts <= 2 * expert_ids.shape[1]
        if near_dense and mesh.shape["node"] == 2 and mesh.shape["local"] % 4 == 0:
            return fused(tokens, expert_ids, route_weights, w_up, w_down)
        return per_device(tokens, expert_ids, route_weights, w_up, w_down)

    return jax.shard_map(
        body,
        mesh=mesh,
        in_specs=placed,
        out_specs=P(("rep", "node", "local"), None),
        check_vma=False,
    )
```

```python
import functools
import jax
import jax.numpy as jnp
from jax import lax
from jax.experimental import pallas as pl
from jax.experimental.pallas import tpu as pltpu
from jax.sharding import PartitionSpec as P

MESH = pl.DeviceIdType.MESH
LANES = 128
LAG_A, LAG_B, LAG_D, LAG_F, LAG_G, LAG_R = 1, 3, 4, 1, 3, 5


def moe_kernel(sizes, x_hbm, ids_ref, weights_ref, up_hbm, down_hbm, out_ref,
               xg, wg, up, down, acc, hid, wcol,
               psend, pown, precv, ysend, yown, yrecv, zsend, zown, zrecv, rin,
               own_sem, up_sem, down_sem,
               gz_s, gz_r, gr_s, go_s, go_r, gy_s, gy_r, gp_s, gp_r,
               rp_s, rp_r, ro_s, ro_r, ry_s, ry_r, rz_s, rz_r, rr_s, rr_r):
    rows, major, chunks, width = sizes
    core = lax.axis_index("node")
    local = lax.axis_index("local")
    z, y = local // 2, lax.rem(local, 2)
    last = major - 1
    low, high = z == 0, z == last
    inner = (z == 1) | (z == last - 1)
    col_rows = major * rows
    half = 2 * col_rows

    def z_plus(d):
        return lax.rem(z + d, major)

    def near(zz):
        return {"local": zz * 2 + y}

    at_y = {"local": z * 2 + (1 - y)}
    at_p = {"node": 1 - core}

    barrier = pltpu.get_barrier_semaphore()
    peers = [near(z_plus(d)) for d in range(1, major)] + [at_y, at_p]
    for peer in peers:
        pl.semaphore_signal(barrier, inc=1, device_id=peer, device_id_type=MESH)

    def rows_of(c, yy, zz):
        return pl.multiple_of(c * half + yy * col_rows + zz * rows, rows)

    mine = rows_of(core, y, z)
    own_x = pltpu.make_async_copy(x_hbm, xg.at[pl.ds(mine, rows), :], own_sem.at[0])
    own_x.start()

    def cols(j):
        return pl.ds(pl.multiple_of(j * width, width), width)

    def up_copy(j):
        return pltpu.make_async_copy(up_hbm.at[0, cols(j), :], up.at[cols(j), :], up_sem.at[j])

    def down_copy(j):
        return pltpu.make_async_copy(down_hbm.at[0, :, cols(j)], down.at[:, cols(j)], down_sem.at[j])

    lax.fori_loop(0, chunks, lambda j, _: (up_copy(j).start(), 0)[1], 0)
    lax.fori_loop(0, chunks, lambda j, _: (down_copy(j).start(), 0)[1], 0)

    lanes = wg.shape[1]
    expert_row = lax.broadcasted_iota(jnp.int32, (lanes, rows), 0)
    spread = jnp.zeros((lanes, rows), jnp.float32)
    for k in range(ids_ref.shape[0]):
        spread += jnp.where(expert_row == ids_ref[k:k + 1, :], weights_ref[k:k + 1, :].astype(jnp.float32), 0.0)
    unit = (lax.broadcasted_iota(jnp.int32, (rows, rows), 0) == lax.broadcasted_iota(jnp.int32, (rows, rows), 1))
    wg[pl.ds(mine, rows), :] = lax.dot_general(
        unit.astype(jnp.float32).astype(jnp.bfloat16), spread.astype(jnp.bfloat16), (((1,), (1,)), ((), ())),
        preferred_element_type=jnp.float32).astype(wg.dtype)

    own_x.wait()
    pl.semaphore_wait(barrier, len(peers))

    def view(start, size, j):
        if j is None:
            return wg.at[pl.ds(start, size), :]
        return xg.at[pl.ds(start, size), cols(j)]

    def idx(j):
        return chunks if j is None else j

    def remote(src, dst, s, r, device):
        return pltpu.make_async_remote_copy(
            src_ref=src, dst_ref=dst, send_sem=s, recv_sem=r, device_id=device, device_id_type=MESH)

    def gz_send(d, j):
        v = view(mine, rows, j)
        return remote(v, v, gz_s.at[d - 1, idx(j)], gz_r.at[d - 1, idx(j)], near(z_plus(d)))

    def direct(d, start):
        if d == 1:
            pl.when(jnp.logical_not(high))(start)
        elif d == last:
            pl.when(jnp.logical_not(low))(start)
        else:
            start()

    def gz_recv(d, j):
        v = view(rows_of(core, y, z_plus(major - d)), rows, j)
        return remote(v, v, gz_s.at[d - 1, idx(j)], gz_r.at[d - 1, idx(j)], near(z_plus(1)))

    far = jnp.where(z == 1, last, 0)
    far_d = jnp.where(z == 1, 2, last - 1)

    def relay(j):
        v = view(rows_of(core, y, far), rows, j)
        d = jnp.where(z == 1, 1, last)
        return remote(v, v, gr_s.at[idx(j)], gz_r.at[d - 1, idx(j)], near(last - far))

    def go(which, j):
        v = view(rows_of(core, which, z), rows, j)
        return remote(v, v, go_s.at[idx(j)], go_r.at[idx(j)], at_y)

    def gy(d, which, j):
        v = view(rows_of(core, which, z_plus(major - d)), rows, j)
        return remote(v, v, gy_s.at[d - 1, idx(j)], gy_r.at[d - 1, idx(j)], at_y)

    def gp(k, c, which, j):
        v = view(rows_of(c, which, 0), col_rows, j)
        return remote(v, v, gp_s.at[k, idx(j)], gp_r.at[k, idx(j)], at_p)

    def stage0(j):
        for d in range(1, major):
            direct(d, lambda: gz_send(d, j).start())
        go(y, j).start()

    def stage_relay(j):
        @pl.when(inner)
        def _():
            gz_recv(far_d, j).wait_recv()
            relay(j).start()

    def stage1(j):
        for d in range(1, major):
            @pl.when(jnp.logical_not(inner & (far_d == d)))
            def _():
                gz_recv(d, j).wait_recv()
            gy(d, y, j).start()
        gp(0, core, y, j).start()

    def stage2(j):
        go(1 - y, j).wait_recv()
        for d in range(1, major):
            gy(d, 1 - y, j).wait_recv()
        gp(1, core, 1 - y, j).start()

    def stage3(j):
        gp(0, 1 - core, y, j).wait_recv()
        gp(1, 1 - core, 1 - y, j).wait_recv()

    lax.fori_loop(0, chunks, lambda j, _: (stage0(j), 0)[1], 0)
    stage0(None)

    def gather_step(t, _):
        @pl.when(t < chunks)
        def _():
            stage_relay(t)

        @pl.when((t >= LAG_A) & (t < chunks + LAG_A))
        def _():
            stage1(t - LAG_A)

        @pl.when((t >= LAG_B) & (t < chunks + LAG_B))
        def _():
            stage2(t - LAG_B)

        @pl.when(t >= LAG_D)
        def _():
            j = t - LAG_D
            stage3(j)
            up_copy(j).wait()
            for k in range(2):
                r = pl.ds(k * half, half)
                part = jnp.dot(xg[r, cols(j)], up[cols(j), :], preferred_element_type=jnp.float32)

                @pl.when(j == 0)
                def _():
                    acc[r, :] = part

                @pl.when(j > 0)
                def _():
                    acc[r, :] += part
        return 0

    lax.fori_loop(0, chunks, gather_step, 0)
    stage_relay(None)
    lax.fori_loop(chunks, chunks + LAG_A, gather_step, 0)
    stage1(None)
    lax.fori_loop(chunks + LAG_A, chunks + LAG_B, gather_step, 0)
    stage2(None)
    lax.fori_loop(chunks + LAG_B, chunks + LAG_D, gather_step, 0)
    stage3(None)

    for k in range(2):
        r = pl.ds(k * half, half)
        v = acc[r, :]
        hid[r, :] = (v / (1.0 + jnp.exp(-v))).astype(hid.dtype)
    expert = core * (2 * major) + local
    lane = lax.broadcasted_iota(jnp.int32, wg.shape, 1)
    wcol[...] = jnp.sum(jnp.where(lane == expert, wg[...].astype(jnp.float32), 0.0), axis=1, keepdims=True)

    def block(zz):
        return pl.ds(pl.multiple_of(zz * rows, rows), rows)

    def rp(j):
        return remote(psend.at[:, cols(j)], precv.at[:, cols(j)], rp_s.at[j], rp_r.at[j], at_p)

    def ry(d, j):
        r = block(z_plus(d))
        return remote(ysend.at[r, cols(j)], yrecv.at[r, cols(j)], ry_s.at[d - 1, j], ry_r.at[d - 1, j], at_y)

    def ro(j):
        return remote(ysend.at[block(z), cols(j)], yrecv.at[block(z), cols(j)], ro_s.at[j], ro_r.at[j], at_y)

    def rz(d, j):
        return remote(zsend.at[block(z_plus(d)), cols(j)], zrecv.at[d - 1, :, cols(j)],
                      rz_s.at[d - 1, j], rz_r.at[d - 1, j], near(z_plus(d)))

    target = last - z
    via = jnp.where(low, 1, last - 1)
    skip_d = jnp.where(z == 1, last - 1, 2)
    goal = jnp.where(z == 1, last, 0)

    def rr(j):
        return remote(zsend.at[block(target), cols(j)], rin.at[:, cols(j)], rr_s.at[j], rr_r.at[j], near(via))

    theirs = pl.ds(pl.multiple_of((1 - core) * half, half), half)
    ours = pl.ds(pl.multiple_of(core * half, half), half)
    y_theirs = pl.ds(pl.multiple_of((1 - y) * col_rows, col_rows), col_rows)
    y_ours = pl.ds(pl.multiple_of(y * col_rows, col_rows), col_rows)

    def wide(ref, r, j):
        return ref[r, cols(j)].astype(jnp.float32)

    def scatter_step(t, _):
        @pl.when(t < chunks)
        def _():
            j = t
            down_copy(j).wait()
            part = jnp.dot(hid[theirs, :], down[:, cols(j)], preferred_element_type=jnp.float32)
            psend[:, cols(j)] = (part * wcol[theirs, :]).astype(psend.dtype)
            rp(j).start()
            part = jnp.dot(hid[ours, :], down[:, cols(j)], preferred_element_type=jnp.float32)
            pown[:, cols(j)] = part * wcol[ours, :]

        @pl.when((t >= LAG_F) & (t < chunks + LAG_F))
        def _():
            j = t - LAG_F
            rp(j).wait_recv()
            ysend[:, cols(j)] = (pown[y_theirs, cols(j)] + wide(precv, y_theirs, j)).astype(ysend.dtype)
            for d in range(1, major):
                ry(d, j).start()
            yown[:, cols(j)] = pown[y_ours, cols(j)] + wide(precv, y_ours, j)

        @pl.when(t == chunks + LAG_F - 1)
        def _():
            lax.fori_loop(0, chunks, lambda i, _: (ro(i).start(), 0)[1], 0)

        @pl.when((t >= LAG_G) & (t < chunks + LAG_G))
        def _():
            j = t - LAG_G
            for d in range(1, major):
                ry(d, j).wait_recv()
                r = block(z_plus(d))
                zsend[r, cols(j)] = (yown[r, cols(j)] + wide(yrecv, r, j)).astype(zsend.dtype)

            @pl.when(low | high)
            def _():
                rr(j).start()
            for d in range(1, major):
                @pl.when(jnp.logical_not(inner & (skip_d == d)))
                def _():
                    direct(d, lambda: rz(d, j).start())

        @pl.when(inner & (t >= LAG_R) & (t < chunks + LAG_R))
        def _():
            j = t - LAG_R
            rr(j).wait_recv()
            zsend[block(goal), cols(j)] = (
                wide(zsend, block(goal), j) + rin[:, cols(j)].astype(jnp.float32)).astype(zsend.dtype)
            for d in range(1, major):
                @pl.when(skip_d == d)
                def _():
                    rz(d, j).start()
        return 0

    lax.fori_loop(0, chunks + LAG_R, scatter_step, 0)

    def finish(j, _):
        ro(j).wait_recv()
        zown[...] = yown[block(z), cols(j)] + wide(yrecv, block(z), j)
        for d in range(1, major):
            def add():
                rz(d, j).wait_recv()
                zown[...] += zrecv[d - 1, :, cols(j)].astype(jnp.float32)
            if d == 1:
                pl.when(jnp.logical_not(low))(add)
            elif d == last:
                pl.when(jnp.logical_not(high))(add)
            else:
                add()
        out_ref[:, cols(j)] = zown[...].astype(out_ref.dtype)
        return 0

    lax.fori_loop(0, chunks, finish, 0)

    def drain_gather(j):
        for d in range(1, major):
            direct(d, lambda: gz_send(d, j).wait_send())
            gy(d, y, j).wait_send()

        @pl.when(inner)
        def _():
            relay(j).wait_send()
        go(y, j).wait_send()
        gp(0, core, y, j).wait_send()
        gp(1, core, 1 - y, j).wait_send()

    def drain(j, _):
        drain_gather(j)
        rp(j).wait_send()
        ro(j).wait_send()
        for d in range(1, major):
            ry(d, j).wait_send()
            direct(d, lambda: rz(d, j).wait_send())

        @pl.when(low | high)
        def _():
            rr(j).wait_send()
        return 0

    drain_gather(None)
    lax.fori_loop(0, chunks, drain, 0)


def fused(tokens, expert_ids, route_weights, w_up, w_down, width=512):
    rows, depth = tokens.shape
    ff = w_up.shape[2]
    experts = lax.axis_size(("node", "local"))
    major = lax.axis_size("local") // 2
    chunks = depth // width
    lanes = -(-experts // LANES) * LANES
    total, col = experts * rows, major * rows
    half = 2 * col
    bf, f32 = jnp.bfloat16, jnp.float32
    dma = pltpu.SemaphoreType.DMA
    return pl.pallas_call(
        functools.partial(moe_kernel, (rows, major, chunks, width)),
        out_shape=jax.ShapeDtypeStruct((rows, depth), bf),
        in_specs=[
            pl.BlockSpec(memory_space=pl.ANY),
            pl.BlockSpec(memory_space=pltpu.VMEM),
            pl.BlockSpec(memory_space=pltpu.VMEM),
            pl.BlockSpec(memory_space=pl.ANY),
            pl.BlockSpec(memory_space=pl.ANY),
        ],
        out_specs=pl.BlockSpec(memory_space=pltpu.VMEM),
        scratch_shapes=[
            pltpu.VMEM((total, depth), bf),
            pltpu.VMEM((total, lanes), bf),
            pltpu.VMEM((depth, ff), bf),
            pltpu.VMEM((ff, depth), bf),
            pltpu.VMEM((total, ff), f32),
            pltpu.VMEM((total, ff), bf),
            pltpu.VMEM((total, 1), f32),
            pltpu.VMEM((half, depth), bf),
            pltpu.VMEM((half, depth), f32),
            pltpu.VMEM((half, depth), bf),
            pltpu.VMEM((col, depth), bf),
            pltpu.VMEM((col, depth), f32),
            pltpu.VMEM((col, depth), bf),
            pltpu.VMEM((col, depth), bf),
            pltpu.VMEM((rows, width), f32),
            pltpu.VMEM((major - 1, rows, depth), bf),
            pltpu.VMEM((rows, depth), bf),
            dma((1,)), dma((chunks,)), dma((chunks,)),
            dma((major - 1, chunks + 1)), dma((major - 1, chunks + 1)), dma((chunks + 1,)),
            dma((chunks + 1,)), dma((chunks + 1,)),
            dma((major - 1, chunks + 1)), dma((major - 1, chunks + 1)),
            dma((2, chunks + 1)), dma((2, chunks + 1)),
            dma((chunks,)), dma((chunks,)),
            dma((chunks,)), dma((chunks,)),
            dma((major - 1, chunks)), dma((major - 1, chunks)),
            dma((major - 1, chunks)), dma((major - 1, chunks)),
            dma((chunks,)), dma((chunks,)),
        ],
        compiler_params=pltpu.CompilerParams(
            collective_id=0, has_side_effects=True, vmem_limit_bytes=60 * 1024 * 1024),
    )(tokens, expert_ids.T, route_weights.T, w_up, w_down)


def place_rows(targets, groups, width):
    onehot = (targets[:, None] == jnp.arange(groups, dtype=jnp.int32)[None, :]).astype(jnp.int32)
    before = jnp.cumsum(onehot, axis=0) - onehot
    rank = jnp.sum(before * onehot, axis=1)
    return jnp.where(targets >= 0, targets * width + rank, groups * width)


def per_device(tokens, expert_ids, route_weights, w_up, w_down):
    up_matrix = w_up[0]
    down_matrix = w_down[0]
    rows = tokens.shape[0]
    top = expert_ids.shape[1]
    width_d = tokens.shape[1]
    experts = lax.axis_size(("node", "local"))
    most = max(4, 2 * rows * top // experts)
    slot = place_rows(expert_ids.reshape(-1), experts, most)
    source = tokens[jnp.arange(rows * top, dtype=jnp.int32) // top]
    buffer = jnp.zeros((experts * most, width_d), jnp.bfloat16).at[slot].set(source, mode="drop")
    buffer = buffer.reshape(experts, most, width_d)
    received = lax.all_to_all(buffer, ("node", "local"), split_axis=0, concat_axis=0, tiled=True)
    shape = received.shape
    flat = received.reshape(-1, shape[-1])
    hidden = jax.nn.silu(jnp.dot(flat, up_matrix, preferred_element_type=jnp.float32)).astype(
        jnp.bfloat16
    )
    answer = jnp.dot(hidden, down_matrix, preferred_element_type=jnp.float32).astype(jnp.bfloat16)
    done = answer.reshape(shape)
    returned = lax.all_to_all(
        done, ("node", "local"), split_axis=0, concat_axis=0, tiled=True
    ).reshape(experts * most, width_d)
    picked = returned[jnp.minimum(slot, experts * most - 1)].reshape(rows, top, width_d)
    mixed = jnp.einsum("tk,tkd->td", route_weights, picked, preferred_element_type=jnp.float32)
    return mixed.astype(jnp.bfloat16)


def solution(mesh):
    placed = (
        P(("rep", "node", "local"), None),
        P(("rep", "node", "local"), None),
        P(("rep", "node", "local"), None),
        P(("node", "local"), None, None),
        P(("node", "local"), None, None),
    )

    def body(tokens, expert_ids, route_weights, w_up, w_down):
        experts = mesh.shape["node"] * mesh.shape["local"]
        near_dense = experts <= 2 * expert_ids.shape[1]
        if near_dense and mesh.shape["node"] == 2 and mesh.shape["local"] % 2 == 0 and mesh.shape["local"] >= 8:
            return fused(tokens, expert_ids, route_weights, w_up, w_down)
        return per_device(tokens, expert_ids, route_weights, w_up, w_down)

    return jax.shard_map(
        body,
        mesh=mesh,
        in_specs=placed,
        out_specs=P(("rep", "node", "local"), None),
        check_vma=False,
    )
```

```python
import functools
import jax
import jax.numpy as jnp
from jax import lax
from jax.experimental import pallas as pl
from jax.experimental.pallas import tpu as pltpu
from jax.sharding import PartitionSpec as P

MESH = pl.DeviceIdType.MESH
LANES = 128
LAG_A, LAG_B, LAG_D, LAG_F, LAG_G, LAG_R = 1, 4, 5, 1, 4, 7
AHEAD = 3


def moe_kernel(sizes, x_hbm, ids_ref, weights_ref, up_hbm, down_hbm, out_ref,
               xg, wg, up, down, acc, hid, wcol,
               psend, pown, precv, ysend, yown, yrecv, zsend, zown, zrecv, rin,
               own_sem, up_sem, down_sem,
               gz_s, gz_r, gr_s, go_s, go_r, gy_s, gy_r, gp_s, gp_r,
               rp_s, rp_r, ro_s, ro_r, ry_s, ry_r, rz_s, rz_r, rr_s, rr_r):
    rows, major, chunks, width = sizes
    core = lax.axis_index("node")
    local = lax.axis_index("local")
    z, y = local // 2, lax.rem(local, 2)
    last = major - 1
    low, high = z == 0, z == last
    inner = (z == 1) | (z == last - 1)
    col_rows = major * rows
    half = 2 * col_rows

    def z_plus(d):
        return lax.rem(z + d, major)

    def near(zz):
        return {"local": zz * 2 + y}

    at_y = {"local": z * 2 + (1 - y)}
    at_p = {"node": 1 - core}

    barrier = pltpu.get_barrier_semaphore()
    peers = [near(z_plus(d)) for d in range(1, major)] + [at_y, at_p]
    for peer in peers:
        pl.semaphore_signal(barrier, inc=1, device_id=peer, device_id_type=MESH)

    def rows_of(c, yy, zz):
        return pl.multiple_of(c * half + yy * col_rows + zz * rows, rows)

    mine = rows_of(core, y, z)
    own_x = pltpu.make_async_copy(x_hbm, xg.at[pl.ds(mine, rows), :], own_sem.at[0])
    own_x.start()

    def cols(j):
        return pl.ds(pl.multiple_of(j * width, width), width)

    def up_copy(j):
        return pltpu.make_async_copy(up_hbm.at[0, cols(j), :], up.at[cols(j), :], up_sem.at[j])

    def down_copy(j):
        return pltpu.make_async_copy(down_hbm.at[0, :, cols(j)], down.at[:, cols(j)], down_sem.at[j])

    lax.fori_loop(0, chunks, lambda j, _: (up_copy(j).start(), 0)[1], 0)
    lax.fori_loop(0, chunks, lambda j, _: (down_copy(j).start(), 0)[1], 0)

    lanes = wg.shape[1]
    expert_row = lax.broadcasted_iota(jnp.int32, (lanes, rows), 0)
    spread = jnp.zeros((lanes, rows), jnp.float32)
    for k in range(ids_ref.shape[0]):
        spread += jnp.where(expert_row == ids_ref[k:k + 1, :], weights_ref[k:k + 1, :].astype(jnp.float32), 0.0)
    unit = (lax.broadcasted_iota(jnp.int32, (rows, rows), 0) == lax.broadcasted_iota(jnp.int32, (rows, rows), 1))
    wg[pl.ds(mine, rows), :] = lax.dot_general(
        unit.astype(jnp.float32).astype(jnp.bfloat16), spread.astype(jnp.bfloat16), (((1,), (1,)), ((), ())),
        preferred_element_type=jnp.float32).astype(wg.dtype)

    own_x.wait()
    pl.semaphore_wait(barrier, len(peers))

    def view(start, size, j):
        if j is None:
            return wg.at[pl.ds(start, size), :]
        return xg.at[pl.ds(start, size), cols(j)]

    def idx(j):
        return chunks if j is None else j

    def remote(src, dst, s, r, device):
        return pltpu.make_async_remote_copy(
            src_ref=src, dst_ref=dst, send_sem=s, recv_sem=r, device_id=device, device_id_type=MESH)

    def gz_send(d, j):
        v = view(mine, rows, j)
        return remote(v, v, gz_s.at[d - 1, idx(j)], gz_r.at[d - 1, idx(j)], near(z_plus(d)))

    def direct(d, start):
        if d == 1:
            pl.when(jnp.logical_not(high))(start)
        elif d == last:
            pl.when(jnp.logical_not(low))(start)
        else:
            start()

    def gz_recv(d, j):
        v = view(rows_of(core, y, z_plus(major - d)), rows, j)
        return remote(v, v, gz_s.at[d - 1, idx(j)], gz_r.at[d - 1, idx(j)], near(z_plus(1)))

    far = jnp.where(z == 1, last, 0)
    far_d = jnp.where(z == 1, 2, last - 1)

    def relay(j):
        v = view(rows_of(core, y, far), rows, j)
        d = jnp.where(z == 1, 1, last)
        return remote(v, v, gr_s.at[idx(j)], gz_r.at[d - 1, idx(j)], near(last - far))

    def go(which, j):
        v = view(rows_of(core, which, z), rows, j)
        return remote(v, v, go_s.at[idx(j)], go_r.at[idx(j)], at_y)

    def gy(d, which, j):
        v = view(rows_of(core, which, z_plus(major - d)), rows, j)
        return remote(v, v, gy_s.at[d - 1, idx(j)], gy_r.at[d - 1, idx(j)], at_y)

    def gp(k, c, which, j):
        v = view(rows_of(c, which, 0), col_rows, j)
        return remote(v, v, gp_s.at[k, idx(j)], gp_r.at[k, idx(j)], at_p)

    def stage0(j):
        for d in (*range(2, last), 1, last):
            direct(d, lambda: gz_send(d, j).start())

    def stage_relay(j):
        @pl.when(inner)
        def _():
            gz_recv(far_d, j).wait_recv()
            relay(j).start()

    def stage1(j):
        for d in range(1, major):
            @pl.when(jnp.logical_not(inner & (far_d == d)))
            def _():
                gz_recv(d, j).wait_recv()
            gy(d, y, j).start()
        gp(0, core, y, j).start()

    def stage2(j):
        go(1 - y, j).wait_recv()
        for d in range(1, major):
            gy(d, 1 - y, j).wait_recv()
        gp(1, core, 1 - y, j).start()

    def stage3(j):
        gp(0, 1 - core, y, j).wait_recv()
        gp(1, 1 - core, 1 - y, j).wait_recv()

    lax.fori_loop(0, AHEAD, lambda j, _: (stage0(j), 0)[1], 0)
    lax.fori_loop(0, chunks, lambda j, _: (go(y, j).start(), 0)[1], 0)
    stage0(None)
    go(y, None).start()

    def gather_step(t, _):
        @pl.when(t + AHEAD < chunks)
        def _():
            stage0(t + AHEAD)

        @pl.when(t < chunks)
        def _():
            stage_relay(t)

        @pl.when((t >= LAG_A) & (t < chunks + LAG_A))
        def _():
            stage1(t - LAG_A)

        @pl.when((t >= LAG_B) & (t < chunks + LAG_B))
        def _():
            stage2(t - LAG_B)

        @pl.when(t >= LAG_D)
        def _():
            j = t - LAG_D
            stage3(j)
            up_copy(j).wait()
            for k in range(2):
                r = pl.ds(k * half, half)
                part = jnp.dot(xg[r, cols(j)], up[cols(j), :], preferred_element_type=jnp.float32)

                @pl.when(j == 0)
                def _():
                    acc[r, :] = part

                @pl.when(j > 0)
                def _():
                    acc[r, :] += part
        return 0

    lax.fori_loop(0, chunks, gather_step, 0)
    stage_relay(None)
    lax.fori_loop(chunks, chunks + LAG_A, gather_step, 0)
    stage1(None)
    lax.fori_loop(chunks + LAG_A, chunks + LAG_B, gather_step, 0)
    stage2(None)
    lax.fori_loop(chunks + LAG_B, chunks + LAG_D, gather_step, 0)
    stage3(None)

    for k in range(2):
        r = pl.ds(k * half, half)
        v = acc[r, :]
        hid[r, :] = (v / (1.0 + jnp.exp(-v))).astype(hid.dtype)
    expert = core * (2 * major) + local
    lane = lax.broadcasted_iota(jnp.int32, wg.shape, 1)
    wcol[...] = jnp.sum(jnp.where(lane == expert, wg[...].astype(jnp.float32), 0.0), axis=1, keepdims=True)

    def block(zz):
        return pl.ds(pl.multiple_of(zz * rows, rows), rows)

    def rp(j):
        return remote(psend.at[:, cols(j)], precv.at[:, cols(j)], rp_s.at[j], rp_r.at[j], at_p)

    def ry(d, j):
        r = block(z_plus(d))
        return remote(ysend.at[r, cols(j)], yrecv.at[r, cols(j)], ry_s.at[d - 1, j], ry_r.at[d - 1, j], at_y)

    def ro(j):
        return remote(ysend.at[block(z), cols(j)], yrecv.at[block(z), cols(j)], ro_s.at[j], ro_r.at[j], at_y)

    def rz(d, j):
        return remote(zsend.at[block(z_plus(d)), cols(j)], zrecv.at[d - 1, :, cols(j)],
                      rz_s.at[d - 1, j], rz_r.at[d - 1, j], near(z_plus(d)))

    target = last - z
    via = jnp.where(low, 1, last - 1)
    skip_d = jnp.where(z == 1, last - 1, 2)
    goal = jnp.where(z == 1, last, 0)

    def rr(j):
        return remote(zsend.at[block(target), cols(j)], rin.at[:, cols(j)], rr_s.at[j], rr_r.at[j], near(via))

    theirs = pl.ds(pl.multiple_of((1 - core) * half, half), half)
    ours = pl.ds(pl.multiple_of(core * half, half), half)
    y_theirs = pl.ds(pl.multiple_of((1 - y) * col_rows, col_rows), col_rows)
    y_ours = pl.ds(pl.multiple_of(y * col_rows, col_rows), col_rows)

    def wide(ref, r, j):
        return ref[r, cols(j)].astype(jnp.float32)

    def scatter_step(t, _):
        @pl.when(t < chunks)
        def _():
            j = t
            down_copy(j).wait()
            part = jnp.dot(hid[theirs, :], down[:, cols(j)], preferred_element_type=jnp.float32)
            psend[:, cols(j)] = (part * wcol[theirs, :]).astype(psend.dtype)
            rp(j).start()
            part = jnp.dot(hid[ours, :], down[:, cols(j)], preferred_element_type=jnp.float32)
            pown[:, cols(j)] = part * wcol[ours, :]

        @pl.when((t >= LAG_F) & (t < chunks + LAG_F))
        def _():
            j = t - LAG_F
            rp(j).wait_recv()
            ysend[:, cols(j)] = (pown[y_theirs, cols(j)] + wide(precv, y_theirs, j)).astype(ysend.dtype)
            for d in range(1, major):
                ry(d, j).start()
            yown[:, cols(j)] = pown[y_ours, cols(j)] + wide(precv, y_ours, j)

        @pl.when(t == chunks + LAG_F - 1)
        def _():
            lax.fori_loop(0, chunks, lambda i, _: (ro(i).start(), 0)[1], 0)

        @pl.when((t >= LAG_G) & (t < chunks + LAG_G))
        def _():
            j = t - LAG_G
            for d in range(1, major):
                ry(d, j).wait_recv()
                r = block(z_plus(d))
                zsend[r, cols(j)] = (yown[r, cols(j)] + wide(yrecv, r, j)).astype(zsend.dtype)

            @pl.when(low | high)
            def _():
                rr(j).start()
            for d in range(1, major):
                @pl.when(jnp.logical_not(inner & (skip_d == d)))
                def _():
                    direct(d, lambda: rz(d, j).start())

        @pl.when(inner & (t >= LAG_R) & (t < chunks + LAG_R))
        def _():
            j = t - LAG_R
            rr(j).wait_recv()
            zsend[block(goal), cols(j)] = (
                wide(zsend, block(goal), j) + rin[:, cols(j)].astype(jnp.float32)).astype(zsend.dtype)
            for d in range(1, major):
                @pl.when(skip_d == d)
                def _():
                    rz(d, j).start()
        return 0

    lax.fori_loop(0, chunks + LAG_R, scatter_step, 0)

    def finish(j, _):
        ro(j).wait_recv()
        zown[...] = yown[block(z), cols(j)] + wide(yrecv, block(z), j)
        for d in range(1, major):
            def add():
                rz(d, j).wait_recv()
                zown[...] += zrecv[d - 1, :, cols(j)].astype(jnp.float32)
            if d == 1:
                pl.when(jnp.logical_not(low))(add)
            elif d == last:
                pl.when(jnp.logical_not(high))(add)
            else:
                add()
        out_ref[:, cols(j)] = zown[...].astype(out_ref.dtype)
        return 0

    lax.fori_loop(0, chunks, finish, 0)

    def drain_gather(j):
        for d in range(1, major):
            direct(d, lambda: gz_send(d, j).wait_send())
            gy(d, y, j).wait_send()

        @pl.when(inner)
        def _():
            relay(j).wait_send()
        go(y, j).wait_send()
        gp(0, core, y, j).wait_send()
        gp(1, core, 1 - y, j).wait_send()

    def drain(j, _):
        drain_gather(j)
        rp(j).wait_send()
        ro(j).wait_send()
        for d in range(1, major):
            ry(d, j).wait_send()
            direct(d, lambda: rz(d, j).wait_send())

        @pl.when(low | high)
        def _():
            rr(j).wait_send()
        return 0

    drain_gather(None)
    lax.fori_loop(0, chunks, drain, 0)


def fused(tokens, expert_ids, route_weights, w_up, w_down, width=512):
    rows, depth = tokens.shape
    ff = w_up.shape[2]
    experts = lax.axis_size(("node", "local"))
    major = lax.axis_size("local") // 2
    chunks = depth // width
    lanes = -(-experts // LANES) * LANES
    total, col = experts * rows, major * rows
    half = 2 * col
    bf, f32 = jnp.bfloat16, jnp.float32
    dma = pltpu.SemaphoreType.DMA
    return pl.pallas_call(
        functools.partial(moe_kernel, (rows, major, chunks, width)),
        out_shape=pltpu.VMEM((rows, depth), bf),
        in_specs=[
            pl.BlockSpec(memory_space=pl.ANY),
            pl.BlockSpec(memory_space=pltpu.VMEM),
            pl.BlockSpec(memory_space=pltpu.VMEM),
            pl.BlockSpec(memory_space=pl.ANY),
            pl.BlockSpec(memory_space=pl.ANY),
        ],
        out_specs=pl.BlockSpec(memory_space=pltpu.VMEM),
        scratch_shapes=[
            pltpu.VMEM((total, depth), bf),
            pltpu.VMEM((total, lanes), bf),
            pltpu.VMEM((depth, ff), bf),
            pltpu.VMEM((ff, depth), bf),
            pltpu.VMEM((total, ff), f32),
            pltpu.VMEM((total, ff), bf),
            pltpu.VMEM((total, 1), f32),
            pltpu.VMEM((half, depth), bf),
            pltpu.VMEM((half, depth), f32),
            pltpu.VMEM((half, depth), bf),
            pltpu.VMEM((col, depth), bf),
            pltpu.VMEM((col, depth), f32),
            pltpu.VMEM((col, depth), bf),
            pltpu.VMEM((col, depth), bf),
            pltpu.VMEM((rows, width), f32),
            pltpu.VMEM((major - 1, rows, depth), bf),
            pltpu.VMEM((rows, depth), bf),
            dma((1,)), dma((chunks,)), dma((chunks,)),
            dma((major - 1, chunks + 1)), dma((major - 1, chunks + 1)), dma((chunks + 1,)),
            dma((chunks + 1,)), dma((chunks + 1,)),
            dma((major - 1, chunks + 1)), dma((major - 1, chunks + 1)),
            dma((2, chunks + 1)), dma((2, chunks + 1)),
            dma((chunks,)), dma((chunks,)),
            dma((chunks,)), dma((chunks,)),
            dma((major - 1, chunks)), dma((major - 1, chunks)),
            dma((major - 1, chunks)), dma((major - 1, chunks)),
            dma((chunks,)), dma((chunks,)),
        ],
        compiler_params=pltpu.CompilerParams(
            collective_id=0, has_side_effects=True, vmem_limit_bytes=60 * 1024 * 1024),
    )(tokens, expert_ids.T, route_weights.T, w_up, w_down)


def place_rows(targets, groups, width):
    onehot = (targets[:, None] == jnp.arange(groups, dtype=jnp.int32)[None, :]).astype(jnp.int32)
    before = jnp.cumsum(onehot, axis=0) - onehot
    rank = jnp.sum(before * onehot, axis=1)
    return jnp.where(targets >= 0, targets * width + rank, groups * width)


def per_device(tokens, expert_ids, route_weights, w_up, w_down):
    up_matrix = w_up[0]
    down_matrix = w_down[0]
    rows = tokens.shape[0]
    top = expert_ids.shape[1]
    width_d = tokens.shape[1]
    experts = lax.axis_size(("node", "local"))
    most = max(4, 2 * rows * top // experts)
    slot = place_rows(expert_ids.reshape(-1), experts, most)
    source = tokens[jnp.arange(rows * top, dtype=jnp.int32) // top]
    buffer = jnp.zeros((experts * most, width_d), jnp.bfloat16).at[slot].set(source, mode="drop")
    buffer = buffer.reshape(experts, most, width_d)
    received = lax.all_to_all(buffer, ("node", "local"), split_axis=0, concat_axis=0, tiled=True)
    shape = received.shape
    flat = received.reshape(-1, shape[-1])
    hidden = jax.nn.silu(jnp.dot(flat, up_matrix, preferred_element_type=jnp.float32)).astype(
        jnp.bfloat16
    )
    answer = jnp.dot(hidden, down_matrix, preferred_element_type=jnp.float32).astype(jnp.bfloat16)
    done = answer.reshape(shape)
    returned = lax.all_to_all(
        done, ("node", "local"), split_axis=0, concat_axis=0, tiled=True
    ).reshape(experts * most, width_d)
    picked = returned[jnp.minimum(slot, experts * most - 1)].reshape(rows, top, width_d)
    mixed = jnp.einsum("tk,tkd->td", route_weights, picked, preferred_element_type=jnp.float32)
    return mixed.astype(jnp.bfloat16)


def solution(mesh):
    placed = (
        P(("rep", "node", "local"), None),
        P(("rep", "node", "local"), None),
        P(("rep", "node", "local"), None),
        P(("node", "local"), None, None),
        P(("node", "local"), None, None),
    )

    def body(tokens, expert_ids, route_weights, w_up, w_down):
        experts = mesh.shape["node"] * mesh.shape["local"]
        near_dense = experts <= 2 * expert_ids.shape[1]
        if near_dense and mesh.shape["node"] == 2 and mesh.shape["local"] % 2 == 0 and mesh.shape["local"] >= 8:
            return fused(tokens, expert_ids, route_weights, w_up, w_down)
        return per_device(tokens, expert_ids, route_weights, w_up, w_down)

    return jax.shard_map(
        body,
        mesh=mesh,
        in_specs=placed,
        out_specs=P(("rep", "node", "local"), None),
        check_vma=False,
    )
```
